512 devices in a mesh: stretch: 4 (over y_lo), seq: 128 (over z, y_hi, x, core).
Axes of the slice: x: 4, y: 8 (y_hi: 2, y_lo: 4; y = y_hi * 4 + y_lo), z: 8, core: 2. Of those that a mesh axis runs over, the one named last changes fastest.
Arguments:
- query_rows: bfloat16 [4, 4096, 4096], P('stretch', 'seq'), may hold values from -160 to 160
- key_rows: bfloat16 [4, 4096, 4096], P('stretch', 'seq'), may hold values from -5 to 5
- value_rows: bfloat16 [4, 4096, 4096], P('stretch', 'seq'), may hold values from -6 to 6
- cache_from: int32 [4], P('stretch'), may hold values from 0 to 4095
- time_index: int32 [4], P('stretch'), may hold values from 0 to 49
- gate_table: float32 [50, 4096], replicated, may hold values from 4 to 16
Outputs:
- attn_out: bfloat16 [4, 4096, 4096], P('stretch', 'seq')
The draws below stay inside these ranges and needn't reach their ends.
All inputs are finite; a program needn't handle non-finite values.
Results may differ from the reference program's by a relative error of at most 0.0055.
Values may be sent and summed in bfloat16 or wider, within the bound.
A program may use at most 64 MiB of HBM per device.

```python
import math
import jax
import jax.numpy as jnp
from jax import lax

HEADS = 32
HD = 128
FEAT = 4096
TOKENS = 4096
CLIPS = 4
NSTEPS = 50


def paired_draw(key):
    base = jax.random.fold_in(key, 17)
    key_draw = jnp.clip(jax.random.normal(jax.random.fold_in(base, 1), (CLIPS, TOKENS, FEAT), jnp.float32), -5.0, 5.0)
    query_draw = jnp.clip(2.0 * jax.random.normal(jax.random.fold_in(base, 2), (CLIPS, TOKENS, FEAT), jnp.float32), -12.0, 12.0)
    return (query_draw, key_draw)


def draw_query_rows(key, part):
    return paired_draw(key)[0].astype(jnp.bfloat16)


def draw_key_rows(key, part):
    return paired_draw(key)[1].astype(jnp.bfloat16)


def with_ends(array, rng, least, high):
    index_at = [jax.random.randint(jax.random.fold_in(rng, axis), (), 0, length) for axis, length in enumerate(array.shape)]
    main_axis = array.shape.index(max(array.shape))
    beside = index_at[:main_axis] + [(index_at[main_axis] + 1) % array.shape[main_axis]] + index_at[main_axis + 1:]
    return array.at[tuple(index_at)].set(least).at[tuple(beside)].set(high)


def levels(stream_key, extent, shards, least, high):
    def one(dim, parts):
        heights = jax.random.uniform(jax.random.fold_in(jax.random.fold_in(stream_key, 6), dim), (parts,), jnp.float32, least / len(shards), high / len(shards))
        return jnp.repeat(jnp.exp(heights), extent[dim] // parts).reshape((-1,) + (1,) * (len(extent) - dim - 1))

    loudness = one(*shards[0])
    for cut in shards[1:]:
        loudness = loudness * one(*cut)
    return loudness


def bell_draw(key, shape, scale, limit, split=(), kind=jnp.bfloat16):
    result = jax.random.normal(key, shape, jnp.float32) * scale
    if len(split) > 0:
        result = levels(key, shape, split, -0.22, 0.18) * result
    return jnp.clip(result, min=-limit, max=limit).astype(kind)


def setup_inputs(seed: int = 0) -> dict:
    key_of = jax.random.split(jax.random.key(seed), 7)
    return {
        "query_rows": draw_query_rows(jax.random.fold_in(key_of[6], 71), 0),
        "key_rows": draw_key_rows(jax.random.fold_in(key_of[6], 71), 0),
        "value_rows": bell_draw(key_of[2], (CLIPS, TOKENS, FEAT), 1.0, 6.0, ((0, 4), (1, 128))),
        "cache_from": with_ends(jax.random.randint(key_of[3], (CLIPS,), 0, TOKENS), jax.random.fold_in(key_of[3], 1), 0, TOKENS - 1).astype(jnp.int32),
        "time_index": with_ends(jax.random.randint(key_of[4], (CLIPS,), 0, NSTEPS), jax.random.fold_in(key_of[4], 1), 0, NSTEPS - 1).astype(jnp.int32),
        "gate_table": jnp.clip(jnp.exp(jax.random.uniform(key_of[5], (NSTEPS, FEAT), jnp.float32, math.log(4.0), math.log(16.0))), 4.0, 16.0),
    }


def attend_head(head_query, head_key, head_value, visible):
    scores = jnp.dot(head_query, head_key.T, preferred_element_type=jnp.float32) * (HD ** -0.5)
    scores = jnp.where(visible[None, :], scores, -1e30)
    largest = jnp.max(scores, axis=1, keepdims=True)
    weights = jnp.where(visible[None, :], jnp.exp(scores - largest), 0.0)
    total = jnp.sum(weights, axis=1, keepdims=True)
    numer = jnp.dot(weights.astype(jnp.bfloat16), head_value, preferred_element_type=jnp.float32)
    return (numer / total).astype(jnp.bfloat16)


def reference(query_rows, key_rows, value_rows, cache_from, time_index, gate_table):
    position = jnp.arange(TOKENS).astype(jnp.int32)
    attn_list = []
    for clip_index in range(CLIPS):
        own_visible = jnp.ones((TOKENS,), bool)
        if clip_index > 0:
            past_key = key_rows[clip_index - 1]
            past_value = value_rows[clip_index - 1]
            past_visible = position >= cache_from[clip_index].astype(jnp.int32)
        else:
            past_key = jnp.zeros_like(key_rows[0])
            past_value = jnp.zeros_like(value_rows[0])
            past_visible = jnp.zeros((TOKENS,), bool)
        visible = jnp.concatenate([own_visible, past_visible])
        keys_all = jnp.concatenate([key_rows[clip_index], past_key], 0).reshape(2 * TOKENS, HEADS, HD).transpose(1, 0, 2)
        values_all = jnp.concatenate([value_rows[clip_index], past_value], 0).reshape(2 * TOKENS, HEADS, HD).transpose(1, 0, 2)
        head_queries = query_rows[clip_index].reshape(TOKENS, HEADS, HD).transpose(1, 0, 2)
        heads_out = lax.map(lambda packed: attend_head(packed[0], packed[1], packed[2], visible), (head_queries, keys_all, values_all))
        attended = heads_out.transpose(1, 0, 2).reshape(TOKENS, FEAT)
        gate_row = gate_table[time_index[clip_index]]
        attn_list.append((attended.astype(jnp.float32) * gate_row).astype(jnp.bfloat16))
    return jnp.stack(attn_list)
```

```python
import functools
import math

import jax
import jax.numpy as jnp
from jax import lax
from jax.experimental import pallas as pl
from jax.experimental.pallas import tpu as pltpu
from jax.sharding import Mesh
from jax.sharding import PartitionSpec as P

HEADS = 32
HD = 128
AXES = ("stretch", "z", "yh", "xh", "xl", "co")
SEQ = AXES[1:]
MESH = pl.DeviceIdType.MESH
NEG = -1e30
LOG2 = HD**-0.5 * math.log2(math.e)
NT = (((1,), (1,)), ((), ()))


def to_row(column):
    return jnp.broadcast_to(column, (128, 128)).T[0:1, :]


def to_column(row):
    return jnp.broadcast_to(row, (128, 128)).T[:, 0:1]


def kernel(
    q_in, k_in, v_in, cf_ref, att,
    q1, k1, v1, qb, qp, kb, vb, cfb, cf_in, bias, op, op_in, st, st_in, ob, r1,
    s1, r1s, l1, s2, r2s, l2, gs, gr, hs, hr, os_, or_, zs, zr, lo, fs, fr, lf,
):
    c, z, yh, xh, xl, co = (lax.axis_index(a) for a in AXES)
    g = yh * 2 + xh
    half = z // 4

    def dev(c=c, z=z, g=g, xl=xl, co=co):
        return (c, z, g // 2, lax.rem(g, 2), xl, co)

    def gx(d):
        return ((yh + d // 2) % 2) * 2 + (xh + d % 2) % 2

    before = lax.rem(c + 3, 4)
    after = lax.rem(c + 1, 4)
    twin = dev(co=1 - co)
    across = dev(xl=1 - xl)

    for slot in range(4):
        vb[slot, :, :, :, HD:] = jnp.ones((8, 4, 32, HD), jnp.bfloat16)
    cfb[...] = jnp.full((8, 128), cf_ref[0], jnp.float32)

    barrier = pltpu.get_barrier_semaphore()
    partners = [dev(z=lax.rem(z + d, 8)) for d in range(1, 8)]
    partners += [dev(g=gx(d)) for d in range(1, 4)]
    partners += [twin, across, dev(c=before), dev(c=after)]
    for partner in partners:
        pl.semaphore_signal(barrier, inc=1, device_id=partner, device_id_type=MESH)
    pl.semaphore_wait(barrier, len(partners))

    def remote(src, dst, send, recv, to):
        return pltpu.make_async_remote_copy(
            src_ref=src, dst_ref=dst, send_sem=send, recv_sem=recv, device_id=to, device_id_type=MESH
        )

    def lanes(start, size):
        return pl.ds(pl.multiple_of(start, 128), size)

    sent = []
    first = []
    for n, (src, dst) in enumerate(((q_in, q1), (k_in, k1), (v_in, v1))):
        copies = [
            remote(src.at[:, lanes(gx(d) * 1024, 1024)], dst.at[g], s1.at[n, d - 1], r1s.at[n, d - 1], dev(g=gx(d)))
            for d in (3, 2, 1)
        ]
        own = pltpu.make_async_copy(src.at[:, lanes(g * 1024, 1024)], dst.at[g], l1.at[n])
        for copy in copies:
            copy.start()
        own.start()
        first.append((copies, own))
        sent += copies

    def second(n, src, dst):
        copies = [
            remote(
                src.at[:, :, lanes(lax.rem(z + d, 8) * HD, HD)], dst(z), s2.at[n, d - 1], r2s.at[n, d - 1],
                dev(z=lax.rem(z + d, 8)),
            )
            for d in (4, 3, 5, 2, 6, 1, 7)
        ]
        own = pltpu.make_async_copy(src.at[:, :, lanes(z * HD, HD)], dst(z), l2.at[n])
        for copy in copies:
            copy.start()
        own.start()
        sent.extend(copies)
        return copies, own

    def arrived(stage):
        copies, own = stage
        for copy in copies:
            copy.wait_recv()
        own.wait()

    def gather(n, buf, cols):
        to_twin = remote(buf.at[0, :, :, :, cols], buf.at[1, :, :, :, cols], gs.at[n, 0], gr.at[n, 0], twin)
        to_across = remote(buf.at[0, :, :, :, cols], buf.at[2, :, :, :, cols], gs.at[n, 1], gr.at[n, 1], across)
        relay = remote(buf.at[2, :, :, :, cols], buf.at[3, :, :, :, cols], gs.at[n, 2], gr.at[n, 2], twin)
        to_across.start()
        to_twin.start()
        sent.extend((to_twin, to_across, relay))
        return to_twin, to_across, relay

    cols = pl.ds(0, HD)
    for slot in range(4):
        vb[slot, :, :, :, HD:] = jnp.ones((8, 4, 32, HD), jnp.bfloat16)
    @pl.when(c == 0)
    def _():
        op_in[...] = jnp.zeros_like(op_in)
        st_in[:, 0:4, :] = jnp.full((2, 4, 128), NEG, jnp.float32)
        st_in[:, 4:8, :] = jnp.zeros((2, 4, 128), jnp.float32)

    arrived(first[0])
    q_stage = second(0, q1, lambda i: qb.at[i])
    arrived(first[1])
    k_stage = second(1, k1, lambda i: kb.at[0, i])
    arrived(q_stage)
    q_hop = remote(qb, qp, hs.at[0], hr.at[0], dev(c=before))
    cf_hop = remote(cfb, cf_in, hs.at[1], hr.at[1], dev(c=before))

    @pl.when(c > 0)
    def _():
        q_hop.start()
        cf_hop.start()

    arrived(first[2])
    v_stage = second(2, v1, lambda i: vb.at[0, i, :, :, cols])
    arrived(k_stage)
    k_twin, k_across, k_relay = gather(0, kb, cols)
    arrived(v_stage)
    v_twin, v_across, v_relay = gather(1, vb, cols)
    k_across.wait_recv()
    k_relay.start()
    k_twin.wait_recv()
    v_across.wait_recv()
    v_relay.start()
    v_twin.wait_recv()
    k_relay.wait_recv()
    v_relay.wait_recv()

    def attend(queries, masked):
        largest = None
        for slot in range(4):
            for part in range(2):
                keys = kb[slot, part * 4 : part * 4 + 4].reshape(512, HD)
                values = vb[slot, part * 4 : part * 4 + 4].reshape(512, 2 * HD)
                scores = lax.dot_general(queries, keys, NT, preferred_element_type=jnp.float32)
                if masked:
                    scores = scores + bias[slot : slot + 1, part * 512 : part * 512 + 512]
                here = jnp.max(scores, axis=1, keepdims=True)
                updated = here if largest is None else jnp.maximum(largest, here)
                weights = jnp.exp2((scores - updated) * LOG2).astype(jnp.bfloat16)
                more = jnp.dot(weights, values, preferred_element_type=jnp.float32)
                numer = more if largest is None else numer * jnp.exp2((largest - updated) * LOG2) + more
                largest = updated
        return largest, numer[:, HD : HD + 1], numer[:, :HD]

    returns = [
        (
            remote(op.at[pl.ds(i * 4, 4)], op_in.at[pl.ds(i * 4, 4)], os_.at[i], or_.at[i], dev(c=after)),
            remote(st.at[i], st_in.at[i], os_.at[2 + i], or_.at[2 + i], dev(c=after)),
        )
        for i in range(2)
    ]

    @pl.when(c < 3)
    def _():
        q_hop.wait_recv()
        cf_hop.wait_recv()
        cache_from = cf_in[0:1, 0:1]
        for slot in range(4):
            chunk = lax.rem(xl + slot // 2, 2) * 2 + lax.rem(co + slot % 2, 2)
            row = lax.broadcasted_iota(jnp.int32, (1, 1024), 1)
            position = (row // 32) * 128 + chunk * 32 + row % 32
            bias[pl.ds(slot, 1), :] = jnp.where(position.astype(jnp.float32) >= cache_from, 0.0, NEG)
        for i in range(2):
            largest, total, numer = attend(qp[i * 4 : i * 4 + 4].reshape(512, HD), True)
            op[pl.ds(i * 4, 4)] = (numer / total).astype(jnp.bfloat16).reshape(4, 4, 32, HD)
            for n in range(4):
                rows = slice(n * 128, n * 128 + 128)
                st[i, n : n + 1, :] = to_row(largest[rows])
                st[i, n + 4 : n + 5, :] = to_row(total[rows])
            for copy in returns[i]:
                copy.start()

    pieces = []

    def pass_on(sender):
        head = (g * 8 + sender) * HD
        for d in (3, 2, 1):
            copy = remote(r1.at[sender, gx(d)], att.at[:, lanes(head, HD)], fs.at[d - 1], fr.at[d - 1], dev(g=gx(d)))
            copy.start()
        pltpu.make_async_copy(r1.at[sender, g], att.at[:, lanes(head, HD)], lf.at[0]).start()

    for i in range(2):
        base = (half + 1 - i) % 2
        rows4 = pl.ds(base * 4, 4)
        largest, total, numer = attend(qb[rows4].reshape(512, HD), False)

        if i == 0:

            @pl.when(c > 0)
            def _():
                for j in range(2):
                    for copy in returns[j]:
                        copy.wait_recv()

        past = op_in[rows4].reshape(512, HD).astype(jnp.float32)
        stats = st_in[base]
        past_largest = jnp.concatenate([to_column(stats[n : n + 1]) for n in range(4)], 0)
        past_total = jnp.concatenate([to_column(stats[n + 4 : n + 5]) for n in range(4)], 0)
        updated = jnp.maximum(largest, past_largest)
        mine = jnp.exp2((largest - updated) * LOG2)
        theirs = past_total * jnp.exp2((past_largest - updated) * LOG2)
        whole = (numer * mine + past * theirs) / (total * mine + theirs)
        ob[rows4] = whole.astype(jnp.bfloat16).reshape(4, 4, 32, HD)
        steps = (0, 1, 2, 3) if i == 0 else (1, 2, 3)
        for k in steps:
            to = base * 4 + (z + k) % 4
            copy = remote(ob.at[to], r1.at[z], zs.at[i * 4 + k], zr.at[z], dev(z=to))
            copy.start()
            pieces.append(copy)
        if i == 1:
            own = pltpu.make_async_copy(ob.at[z], r1.at[z], lo.at[0])
            own.start()
        for k in steps:
            sender = base * 4 + (z + k) % 4
            remote(ob.at[0], r1.at[sender], zs.at[0], zr.at[sender], dev(z=sender)).wait_recv()
            pass_on(sender)
        if i == 1:
            own.wait()
            pass_on(z)

    all_rows = att.at[:, pl.ds(0, 1024)]
    pltpu.make_async_copy(all_rows, all_rows, lf.at[0]).wait()
    for d in (1, 2, 3):
        remote(all_rows, all_rows, fs.at[d - 1], fr.at[d - 1], twin).wait()
    for copy in sent + pieces:
        copy.wait_send()

    @pl.when(c > 0)
    def _():
        q_hop.wait_send()
        cf_hop.wait_send()

    @pl.when(c < 3)
    def _():
        for i in range(2):
            for copy in returns[i]:
                copy.wait_send()


def body(query_rows, key_rows, value_rows, cache_from, time_index, gate_table):
    bf16, f32, dma = jnp.bfloat16, jnp.float32, pltpu.SemaphoreType.DMA
    vmem = pl.BlockSpec(memory_space=pltpu.VMEM)
    hbm = pl.BlockSpec(memory_space=pltpu.HBM)
    attended = pl.pallas_call(
        kernel,
        out_shape=jax.ShapeDtypeStruct((32, HEADS * HD), bf16),
        in_specs=[hbm, hbm, hbm, pl.BlockSpec(memory_space=pltpu.SMEM)],
        out_specs=vmem,
        scratch_shapes=[
            *[pltpu.VMEM((4, 32, 1024), bf16)] * 3,
            *[pltpu.VMEM((8, 4, 32, HD), bf16)] * 2,
            pltpu.VMEM((4, 8, 4, 32, HD), bf16),
            pltpu.VMEM((4, 8, 4, 32, 2 * HD), bf16),
            *[pltpu.VMEM((8, 128), f32)] * 2,
            pltpu.VMEM((8, 1024), f32),
            *[pltpu.VMEM((8, 4, 32, HD), bf16)] * 2,
            *[pltpu.VMEM((2, 8, 128), f32)] * 2,
            *[pltpu.VMEM((8, 4, 32, HD), bf16)] * 2,
            dma((3, 3)), dma((3, 3)), dma((3,)),
            dma((3, 7)), dma((3, 7)), dma((3,)),
            dma((2, 3)), dma((2, 3)),
            dma((2,)), dma((2,)),
            dma((4,)), dma((4,)),
            dma((8,)), dma((8,)), dma((1,)),
            dma((3,)), dma((3,)), dma((1,)),
        ],
        compiler_params=pltpu.CompilerParams(
            collective_id=1, has_side_effects=True
        ),
    )(query_rows[0], key_rows[0], value_rows[0], cache_from)
    gate_row = lax.dynamic_slice_in_dim(gate_table, time_index[0], 1, 0)
    return (attended.astype(jnp.float32) * gate_row).astype(jnp.bfloat16)[None]


def solution(mesh):
    finer = Mesh(mesh.devices.reshape(4, 8, 2, 2, 2, 2), AXES)
    rows = P("stretch", SEQ, None)
    return jax.shard_map(
        body,
        mesh=finer,
        in_specs=(rows, rows, rows, P("stretch"), P("stretch"), P()),
        out_specs=rows,
        check_vma=False,
    )
```

```python
import functools
import math

import jax
import jax.numpy as jnp
from jax import lax
from jax.experimental import pallas as pl
from jax.experimental.pallas import tpu as pltpu
from jax.sharding import Mesh
from jax.sharding import PartitionSpec as P

HEADS = 32
HD = 128
AXES = ("stretch", "z", "yh", "xh", "xl", "co")
SEQ = AXES[1:]
MESH = pl.DeviceIdType.MESH
NEG = -1e30
LOG2 = HD**-0.5 * math.log2(math.e)
NT = (((1,), (1,)), ((), ()))


def to_row(column):
    return jnp.broadcast_to(column, (128, 128)).T[0:1, :]


def to_column(row):
    return jnp.broadcast_to(row, (128, 128)).T[:, 0:1]


def kernel(
    q_in, k_in, v_in, cf_ref, att,
    qb, qp, kb, vb, cfb, cf_in, bias, held, held_max, op, op_in, st, st_in, ob,
    meet, asend, arecv, alocal, gs, gr, hs, hr, os_, or_, rs, rr, rl,
):
    c, z, yh, xh, xl, co = (lax.axis_index(a) for a in AXES)
    g = yh * 2 + xh
    half = z // 4
    head = z * 4 + g

    def dev(c=c, z=z, g=g, xl=xl, co=co):
        return (c, z, g // 2, lax.rem(g, 2), xl, co)

    def gx(d):
        return ((yh + d // 2) % 2) * 2 + (xh + d % 2) % 2

    def zx(d):
        return lax.rem(z + d, 8)

    before = lax.rem(c + 3, 4)
    after = lax.rem(c + 1, 4)
    twin = dev(co=1 - co)
    across = dev(xl=1 - xl)

    def signal(semaphore, partners):
        for partner in partners:
            pl.semaphore_signal(semaphore, inc=1, device_id=partner, device_id_type=MESH)

    barrier = pltpu.get_barrier_semaphore()
    line = [dev(z=zx(d)) for d in (4, 3, 5, 2, 6, 1, 7)]
    others = [dev(g=gx(d)) for d in (3, 2, 1)]
    near = [dev(c=before), dev(c=after), across, twin]
    signal(barrier, line + others + near)
    for slot in range(4):
        vb[slot, :, :, :, HD:] = jnp.ones((8, 4, 32, HD), jnp.bfloat16)
    cfb[...] = jnp.full((8, 128), cf_ref[0], jnp.float32)
    pl.semaphore_wait(barrier, len(line + others + near))
    signal(meet, others)
    pl.semaphore_wait(meet, len(others))

    def remote(src, dst, send, recv, to):
        return pltpu.make_async_remote_copy(
            src_ref=src, dst_ref=dst, send_sem=send, recv_sem=recv, device_id=to, device_id_type=MESH
        )

    def lanes(start, size):
        return pl.ds(pl.multiple_of(start, 128), size)

    sent = []
    far = [(d, e) for d in (4, 3, 5, 2, 6, 1, 7, 0) for e in (3, 2, 1, 0) if (d, e) != (0, 0)]

    def exchange(n, src, dst):
        for d, e in far:
            to_z, to_g = zx(d), gx(e)
            remote(
                src.at[:, lanes((to_z * 4 + to_g) * HD, HD)], dst, asend.at[n], arecv.at[n], dev(z=to_z, g=to_g)
            ).start()
        pltpu.make_async_copy(src.at[:, lanes(head * HD, HD)], dst, alocal.at[n]).start()

    def all_bytes(semaphore):
        area = att.at[:, pl.ds(0, len(far) * HD)]
        return pltpu.make_async_copy(area, area, semaphore)

    def arrived(n):
        all_bytes(arecv.at[n]).wait()
        area = att.at[:, pl.ds(0, HD)]
        pltpu.make_async_copy(area, area, alocal.at[n]).wait()

    def gather(n, buf, cols):
        to_twin = remote(buf.at[0, :, :, :, cols], buf.at[1, :, :, :, cols], gs.at[n, 0], gr.at[n, 0], twin)
        to_across = remote(buf.at[0, :, :, :, cols], buf.at[2, :, :, :, cols], gs.at[n, 1], gr.at[n, 1], across)
        relay = remote(buf.at[2, :, :, :, cols], buf.at[3, :, :, :, cols], gs.at[n, 2], gr.at[n, 2], twin)
        to_across.start()
        to_twin.start()
        sent.extend((to_twin, to_across, relay))
        return to_twin, to_across, relay

    cols = pl.ds(0, HD)
    for slot in range(4):
        vb[slot, :, :, :, HD:] = jnp.ones((8, 4, 32, HD), jnp.bfloat16)
    @pl.when(c == 0)
    def _():
        op_in[...] = jnp.zeros_like(op_in)
        st_in[:, 0:4, :] = jnp.full((2, 4, 128), NEG, jnp.float32)
        st_in[:, 4:8, :] = jnp.zeros((2, 4, 128), jnp.float32)

    exchange(0, q_in, qb.at[z, g])
    exchange(1, k_in, kb.at[0, z, g])
    exchange(2, v_in, vb.at[0, z, g, :, cols])

    arrived(0)
    q_hop = remote(qb, qp, hs.at[0], hr.at[0], dev(c=before))
    cf_hop = remote(cfb, cf_in, hs.at[1], hr.at[1], dev(c=before))

    @pl.when(c > 0)
    def _():
        q_hop.start()
        cf_hop.start()

    arrived(1)
    k_twin, k_across, k_relay = gather(0, kb, cols)
    arrived(2)
    v_twin, v_across, v_relay = gather(1, vb, cols)
    k_across.wait_recv()
    k_relay.start()
    k_twin.wait_recv()
    v_twin.wait_recv()

    def attend(queries, slots, masked, state=None):
        largest, numer = state if state else (None, None)
        for slot in slots:
            for part in range(2):
                keys = kb[slot, part * 4 : part * 4 + 4].reshape(512, HD)
                values = vb[slot, part * 4 : part * 4 + 4].reshape(512, 2 * HD)
                scores = lax.dot_general(queries, keys, NT, preferred_element_type=jnp.float32)
                if masked:
                    scores = scores + bias[slot : slot + 1, part * 512 : part * 512 + 512]
                here = jnp.max(scores, axis=1, keepdims=True)
                updated = here if largest is None else jnp.maximum(largest, here)
                weights = jnp.exp2((scores - updated) * LOG2).astype(jnp.bfloat16)
                more = jnp.dot(weights, values, preferred_element_type=jnp.float32)
                numer = more if largest is None else numer * jnp.exp2((largest - updated) * LOG2) + more
                largest = updated
        return largest, numer

    returns = [
        (
            remote(op.at[pl.ds(i * 4, 4)], op_in.at[pl.ds(i * 4, 4)], os_.at[i], or_.at[i], dev(c=after)),
            remote(st.at[i], st_in.at[i], os_.at[2 + i], or_.at[2 + i], dev(c=after)),
        )
        for i in range(2)
    ]

    def past_queries(i):
        return qp[i * 4 : i * 4 + 4].reshape(512, HD)

    def past_begin(i):
        largest, numer = attend(past_queries(i), (0, 1), True)
        held[i] = numer
        held_max[i] = jnp.broadcast_to(largest, (512, 128))

    @pl.when(c < 3)
    def _():
        q_hop.wait_recv()
        cf_hop.wait_recv()
        cache_from = cf_in[0:1, 0:1]
        for slot in range(4):
            chunk = lax.rem(xl + slot // 2, 2) * 2 + lax.rem(co + slot % 2, 2)
            row = lax.broadcasted_iota(jnp.int32, (1, 1024), 1)
            position = (row // 32) * 128 + chunk * 32 + row % 32
            bias[pl.ds(slot, 1), :] = jnp.where(position.astype(jnp.float32) >= cache_from, 0.0, NEG)
        past_begin(0)

    v_across.wait_recv()
    v_relay.start()

    @pl.when(c < 3)
    def _():
        past_begin(1)

    k_relay.wait_recv()
    v_relay.wait_recv()

    @pl.when(c < 3)
    def _():
        for i in range(2):
            largest, numer = attend(past_queries(i), (2, 3), True, (held_max[i][:, 0:1], held[i]))
            total = numer[:, HD : HD + 1]
            op[pl.ds(i * 4, 4)] = (numer[:, :HD] / total).astype(jnp.bfloat16).reshape(4, 4, 32, HD)
            for n in range(4):
                rows = slice(n * 128, n * 128 + 128)
                st[i, n : n + 1, :] = to_row(largest[rows])
                st[i, n + 4 : n + 5, :] = to_row(total[rows])
            for copy in returns[i]:
                copy.start()

    for i in range(2):
        base = (half + 1 - i) % 2
        rows4 = pl.ds(base * 4, 4)
        largest, numer = attend(qb[rows4].reshape(512, HD), (0, 1, 2, 3), False)
        total = numer[:, HD : HD + 1]

        if i == 0:

            @pl.when(c > 0)
            def _():
                for j in range(2):
                    for copy in returns[j]:
                        copy.wait_recv()

        past = op_in[rows4].reshape(512, HD).astype(jnp.float32)
        stats = st_in[base]
        past_largest = jnp.concatenate([to_column(stats[n : n + 1]) for n in range(4)], 0)
        past_total = jnp.concatenate([to_column(stats[n + 4 : n + 5]) for n in range(4)], 0)
        updated = jnp.maximum(largest, past_largest)
        mine = jnp.exp2((largest - updated) * LOG2)
        theirs = past_total * jnp.exp2((past_largest - updated) * LOG2)
        whole = (numer[:, :HD] * mine + past * theirs) / (total * mine + theirs)
        ob[rows4] = whole.astype(jnp.bfloat16).reshape(4, 4, 32, HD)
        for k in range(4):
            to_z = base * 4 + (z + k) % 4
            for e in (3, 2, 1, 0):
                to_g = gx(e)
                if i == 1 and k == 0 and e == 0:
                    continue
                remote(
                    ob.at[to_z, to_g], att.at[:, lanes(head * HD, HD)], rs.at[0], rr.at[0], dev(z=to_z, g=to_g)
                ).start()
    own = pltpu.make_async_copy(ob.at[z, g], att.at[:, lanes(head * HD, HD)], rl.at[0])
    own.start()
    own.wait()
    all_bytes(rr.at[0]).wait()
    all_bytes(rs.at[0]).wait()
    for n in range(3):
        all_bytes(asend.at[n]).wait()
    for copy in sent:
        copy.wait_send()

    @pl.when(c > 0)
    def _():
        q_hop.wait_send()
        cf_hop.wait_send()

    @pl.when(c < 3)
    def _():
        for i in range(2):
            for copy in returns[i]:
                copy.wait_send()


def body(query_rows, key_rows, value_rows, cache_from, time_index, gate_table):
    bf16, f32, dma = jnp.bfloat16, jnp.float32, pltpu.SemaphoreType.DMA
    vmem = pl.BlockSpec(memory_space=pltpu.VMEM)
    hbm = pl.BlockSpec(memory_space=pltpu.HBM)
    attended = pl.pallas_call(
        kernel,
        out_shape=jax.ShapeDtypeStruct((32, HEADS * HD), bf16),
        in_specs=[hbm, hbm, hbm, pl.BlockSpec(memory_space=pltpu.SMEM)],
        out_specs=vmem,
        scratch_shapes=[
            *[pltpu.VMEM((8, 4, 32, HD), bf16)] * 2,
            pltpu.VMEM((4, 8, 4, 32, HD), bf16),
            pltpu.VMEM((4, 8, 4, 32, 2 * HD), bf16),
            *[pltpu.VMEM((8, 128), f32)] * 2,
            pltpu.VMEM((8, 1024), f32),
            pltpu.VMEM((2, 512, 2 * HD), f32),
            pltpu.VMEM((2, 512, 128), f32),
            *[pltpu.VMEM((8, 4, 32, HD), bf16)] * 2,
            *[pltpu.VMEM((2, 8, 128), f32)] * 2,
            pltpu.VMEM((8, 4, 32, HD), bf16),
            pltpu.SemaphoreType.REGULAR,
            *[dma((3,))] * 3,
            *[dma((2, 3))] * 2,
            *[dma((2,))] * 2,
            *[dma((4,))] * 2,
            *[dma((1,))] * 3,
        ],
        compiler_params=pltpu.CompilerParams(
            collective_id=1, has_side_effects=True
        ),
    )(query_rows[0], key_rows[0], value_rows[0], cache_from)
    gate_row = lax.dynamic_slice_in_dim(gate_table, time_index[0], 1, 0)
    return (attended.astype(jnp.float32) * gate_row).astype(jnp.bfloat16)[None]


def solution(mesh):
    finer = Mesh(mesh.devices.reshape(4, 8, 2, 2, 2, 2), AXES)
    rows = P("stretch", SEQ, None)
    return jax.shard_map(
        body,
        mesh=finer,
        in_specs=(rows, rows, rows, P("stretch"), P("stretch"), P()),
        out_specs=rows,
        check_vma=False,
    )
```

```python
import functools
import math

import jax
import jax.numpy as jnp
from jax import lax
from jax.experimental import pallas as pl
from jax.experimental.pallas import tpu as pltpu
from jax.sharding import Mesh
from jax.sharding import PartitionSpec as P

HEADS = 32
HD = 128
AXES = ("stretch", "z", "yh", "xh", "xl", "co")
SEQ = AXES[1:]
MESH = pl.DeviceIdType.MESH
NEG = -1e30
LOG2 = HD**-0.5 * math.log2(math.e)
NT = (((1,), (1,)), ((), ()))


def to_row(column):
    return jnp.broadcast_to(column, (128, 128)).T[0:1, :]


def to_column(row):
    return jnp.broadcast_to(row, (128, 128)).T[:, 0:1]


def kernel(
    q_in, k_in, v_in, cf_ref, att,
    qb, qp, kb, vb, cfb, cf_in, bias, held, held_max, op, op_in, st, st_in, ob,
    asend, arecv, alocal, gs, gr, hs, hr, os_, or_, rs, rr, rl,
):
    c, z, yh, xh, xl, co = (lax.axis_index(a) for a in AXES)
    g = yh * 2 + xh
    half = z // 4
    head = z * 4 + g

    def dev(c=c, z=z, g=g, xl=xl, co=co):
        return (c, z, g // 2, lax.rem(g, 2), xl, co)

    def gx(d):
        return ((yh + d // 2) % 2) * 2 + (xh + d % 2) % 2

    def zx(d):
        return lax.rem(z + d, 8)

    before = lax.rem(c + 3, 4)
    after = lax.rem(c + 1, 4)
    twin = dev(co=1 - co)
    across = dev(xl=1 - xl)

    far = sorted(
        ((d, e) for d in range(8) for e in range(4) if (d, e) != (0, 0)),
        key=lambda p: -(min(p[0], 8 - p[0]) + 4 * (p[1] // 2) + 2 * (p[1] % 2)),
    )
    barrier = pltpu.get_barrier_semaphore()
    partners = [dev(z=zx(d), g=gx(e)) for d, e in far]
    partners += [dev(c=before), dev(c=after), across, twin]
    for partner in partners:
        pl.semaphore_signal(barrier, inc=1, device_id=partner, device_id_type=MESH)
    for slot in range(4):
        vb[slot, :, :, :, :, HD:] = jnp.ones((2, 8, 4, 16, HD), jnp.bfloat16)
    cfb[...] = jnp.full((8, 128), cf_ref[0], jnp.float32)
    pl.semaphore_wait(barrier, len(partners))

    def remote(src, dst, send, recv, to):
        return pltpu.make_async_remote_copy(
            src_ref=src, dst_ref=dst, send_sem=send, recv_sem=recv, device_id=to, device_id_type=MESH
        )

    def lanes(start, size):
        return pl.ds(pl.multiple_of(start, 128), size)

    sent = []

    def exchange(n, rows, src, dst):
        for d, e in far:
            to_z, to_g = zx(d), gx(e)
            remote(
                src.at[rows, lanes((to_z * 4 + to_g) * HD, HD)], dst, asend.at[n], arecv.at[n], dev(z=to_z, g=to_g)
            ).start()
        pltpu.make_async_copy(src.at[rows, lanes(head * HD, HD)], dst, alocal.at[n]).start()

    def all_bytes(semaphore, rows=32):
        area = att.at[0:rows, pl.ds(0, len(far) * HD)]
        return pltpu.make_async_copy(area, area, semaphore)

    def arrived(n, rows=16):
        all_bytes(arecv.at[n], rows).wait()
        area = att.at[0:rows, pl.ds(0, HD)]
        pltpu.make_async_copy(area, area, alocal.at[n]).wait()

    def gather(n, part, buf):
        at = [buf.at[slot, part, :, :, :, cols] for slot in range(4)]
        to_twin = remote(at[0], at[1], gs.at[n, 0], gr.at[n, 0], twin)
        to_across = remote(at[0], at[2], gs.at[n, 1], gr.at[n, 1], across)
        relay = remote(at[2], at[3], gs.at[n, 2], gr.at[n, 2], twin)
        to_across.start()
        to_twin.start()
        sent.extend((to_twin, to_across, relay))
        return to_twin, to_across, relay

    cols = pl.ds(0, HD)
    for slot in range(4):
        vb[slot, :, :, :, :, HD:] = jnp.ones((2, 8, 4, 16, HD), jnp.bfloat16)
    @pl.when(c == 0)
    def _():
        op_in[...] = jnp.zeros_like(op_in)
        st_in[:, 0:4, :] = jnp.full((2, 4, 128), NEG, jnp.float32)
        st_in[:, 4:8, :] = jnp.zeros((2, 4, 128), jnp.float32)

    exchange(0, pl.ds(0, 32), q_in, qb.at[z, g])
    for part in range(2):
        rows = pl.ds(part * 16, 16)
        exchange(1 + 2 * part, rows, k_in, kb.at[0, part, z, g])
        exchange(2 + 2 * part, rows, v_in, vb.at[0, part, z, g, :, cols])

    arrived(0, 32)
    q_hop = remote(qb, qp, hs.at[0], hr.at[0], dev(c=before))
    cf_hop = remote(cfb, cf_in, hs.at[1], hr.at[1], dev(c=before))

    @pl.when(c > 0)
    def _():
        cf_hop.start()
        q_hop.start()

    here_0, here_1, there_0, there_1 = (((s, p), (s + 1, p)) for s in (0, 2) for p in (0, 1))

    def attend(queries, groups, masked, state=None):
        largest, numer = state if state else (None, None)
        for slot, part in groups:
            keys = kb[slot, part].reshape(512, HD)
            values = vb[slot, part].reshape(512, 2 * HD)
            scores = lax.dot_general(queries, keys, NT, preferred_element_type=jnp.float32)
            if masked:
                scores = scores + bias[slot : slot + 1, part * 512 : part * 512 + 512]
            top = jnp.max(scores, axis=1, keepdims=True)
            updated = top if largest is None else jnp.maximum(largest, top)
            weights = jnp.exp2((scores - updated) * LOG2).astype(jnp.bfloat16)
            more = jnp.dot(weights, values, preferred_element_type=jnp.float32)
            numer = more if largest is None else numer * jnp.exp2((largest - updated) * LOG2) + more
            largest = updated
        return largest, numer

    def hold(n, result):
        held_max[n] = jnp.broadcast_to(result[0], (512, 128))
        held[n] = result[1]

    def holding(n):
        return held_max[n][:, 0:1], held[n]

    def queries_of(buf, i):
        return buf[pl.ds(((half + 1 - i) % 2) * 4, 4)].reshape(512, HD)

    def past_more(groups):
        @pl.when(c < 3)
        def _():
            for i in range(2):
                hold(i, attend(queries_of(qp, i), groups, True, holding(i)))

    def returns(i):
        rows4 = pl.ds(((half + 1 - i) % 2) * 4, 4)
        return (
            remote(op.at[rows4], op_in.at[rows4], os_.at[i], or_.at[i], dev(c=after)),
            remote(st.at[i], st_in.at[i], os_.at[2 + i], or_.at[2 + i], dev(c=after)),
        )

    arrived(1)
    k0_twin, k0_across, k0_relay = gather(0, 0, kb)
    arrived(2)
    v0_twin, v0_across, v0_relay = gather(1, 0, vb)
    k0_across.wait_recv()
    k0_relay.start()
    k0_twin.wait_recv()
    v0_twin.wait_recv()
    hold(2, attend(queries_of(qb, 0), here_0, False))
    arrived(3)
    k1_twin, k1_across, k1_relay = gather(2, 1, kb)
    v0_across.wait_recv()
    v0_relay.start()

    @pl.when(c < 3)
    def _():
        q_hop.wait_recv()
        cf_hop.wait_recv()
        cache_from = cf_in[0:1, 0:1]
        for slot in range(4):
            chunk = lax.rem(xl + slot // 2, 2) * 2 + lax.rem(co + slot % 2, 2)
            row = lax.broadcasted_iota(jnp.int32, (1, 1024), 1)
            position = ((row % 512) // 16) * 128 + chunk * 32 + (row // 512) * 16 + row % 16
            bias[pl.ds(slot, 1), :] = jnp.where(position.astype(jnp.float32) >= cache_from, 0.0, NEG)
        for i in range(2):
            hold(i, attend(queries_of(qp, i), here_0, True))

    arrived(4)
    v1_twin, v1_across, v1_relay = gather(3, 1, vb)
    k0_relay.wait_recv()
    v0_relay.wait_recv()
    past_more(there_0)
    k1_across.wait_recv()
    k1_relay.start()
    k1_twin.wait_recv()
    v1_twin.wait_recv()
    past_more(here_1)
    v1_across.wait_recv()
    v1_relay.start()
    hold(3, attend(queries_of(qb, 1), here_0, False))
    k1_relay.wait_recv()
    v1_relay.wait_recv()

    @pl.when(c < 3)
    def _():
        for i in range(2):
            largest, numer = attend(queries_of(qp, i), there_1, True, holding(i))
            total = numer[:, HD : HD + 1]
            rows4 = pl.ds(((half + 1 - i) % 2) * 4, 4)
            op[rows4] = (numer[:, :HD] / total).astype(jnp.bfloat16).reshape(4, 4, 32, HD)
            for n in range(4):
                rows = slice(n * 128, n * 128 + 128)
                st[i, n : n + 1, :] = to_row(largest[rows])
                st[i, n + 4 : n + 5, :] = to_row(total[rows])
            for copy in returns(i):
                copy.start()

    for i in range(2):
        base = (half + 1 - i) % 2
        rows4 = pl.ds(base * 4, 4)
        largest, numer = attend(queries_of(qb, i), there_0 + here_1 + there_1, False, holding(2 + i))
        total = numer[:, HD : HD + 1]

        @pl.when(c > 0)
        def _():
            for copy in returns(i):
                copy.wait_recv()

        past = op_in[rows4].reshape(512, HD).astype(jnp.float32)
        past_largest = jnp.concatenate([to_column(st_in[i, n : n + 1, :]) for n in range(4)], 0)
        past_total = jnp.concatenate([to_column(st_in[i, n + 4 : n + 5, :]) for n in range(4)], 0)
        updated = jnp.maximum(largest, past_largest)
        mine = jnp.exp2((largest - updated) * LOG2)
        theirs = past_total * jnp.exp2((past_largest - updated) * LOG2)
        whole = (numer[:, :HD] * mine + past * theirs) / (total * mine + theirs)
        ob[rows4] = whole.astype(jnp.bfloat16).reshape(4, 4, 32, HD)
        for k in range(4):
            to_z = base * 4 + (z + k) % 4
            for e in (3, 2, 1, 0):
                to_g = gx(e)
                if i == 1 and k == 0 and e == 0:
                    continue
                remote(
                    ob.at[to_z, to_g], att.at[:, lanes(head * HD, HD)], rs.at[0], rr.at[0], dev(z=to_z, g=to_g)
                ).start()
    own = pltpu.make_async_copy(ob.at[z, g], att.at[:, lanes(head * HD, HD)], rl.at[0])
    own.start()
    own.wait()
    all_bytes(rr.at[0]).wait()
    all_bytes(rs.at[0]).wait()
    for n in range(5):
        all_bytes(asend.at[n], 16 if n else 32).wait()
    for copy in sent:
        copy.wait_send()

    @pl.when(c > 0)
    def _():
        q_hop.wait_send()
        cf_hop.wait_send()

    @pl.when(c < 3)
    def _():
        for i in range(2):
            for copy in returns(i):
                copy.wait_send()


def body(query_rows, key_rows, value_rows, cache_from, time_index, gate_table):
    bf16, f32, dma = jnp.bfloat16, jnp.float32, pltpu.SemaphoreType.DMA
    vmem = pl.BlockSpec(memory_space=pltpu.VMEM)
    hbm = pl.BlockSpec(memory_space=pltpu.HBM)
    attended = pl.pallas_call(
        kernel,
        out_shape=jax.ShapeDtypeStruct((32, HEADS * HD), bf16),
        in_specs=[hbm, hbm, hbm, pl.BlockSpec(memory_space=pltpu.SMEM)],
        out_specs=vmem,
        scratch_shapes=[
            *[pltpu.VMEM((8, 4, 32, HD), bf16)] * 2,
            pltpu.VMEM((4, 2, 8, 4, 16, HD), bf16),
            pltpu.VMEM((4, 2, 8, 4, 16, 2 * HD), bf16),
            *[pltpu.VMEM((8, 128), f32)] * 2,
            pltpu.VMEM((8, 1024), f32),
            pltpu.VMEM((4, 512, 2 * HD), f32),
            pltpu.VMEM((4, 512, 128), f32),
            *[pltpu.VMEM((8, 4, 32, HD), bf16)] * 2,
            *[pltpu.VMEM((2, 8, 128), f32)] * 2,
            pltpu.VMEM((8, 4, 32, HD), bf16),
            *[dma((5,))] * 3,
            *[dma((4, 3))] * 2,
            *[dma((2,))] * 2,
            *[dma((4,))] * 2,
            *[dma((1,))] * 3,
        ],
        compiler_params=pltpu.CompilerParams(
            collective_id=1, has_side_effects=True
        ),
    )(query_rows[0], key_rows[0], value_rows[0], cache_from)
    gate_row = lax.dynamic_slice_in_dim(gate_table, time_index[0], 1, 0)
    return (attended.astype(jnp.float32) * gate_row).astype(jnp.bfloat16)[None]


def solution(mesh):
    finer = Mesh(mesh.devices.reshape(4, 8, 2, 2, 2, 2), AXES)
    rows = P("stretch", SEQ, None)
    return jax.shard_map(
        body,
        mesh=finer,
        in_specs=(rows, rows, rows, P("stretch"), P("stretch"), P()),
        out_specs=rows,
        check_vma=False,
    )
```

```python
import functools
import math

import jax
import jax.numpy as jnp
from jax import lax
from jax.experimental import pallas as pl
from jax.experimental.pallas import tpu as pltpu
from jax.sharding import Mesh
from jax.sharding import PartitionSpec as P

HEADS = 32
HD = 128
AXES = ("stretch", "z", "yh", "xh", "xl", "co")
SEQ = AXES[1:]
MESH = pl.DeviceIdType.MESH
NEG = -1e30
LOG2 = HD**-0.5 * math.log2(math.e)
NT = (((1,), (1,)), ((), ()))


def to_row(column):
    return jnp.broadcast_to(column, (128, 128)).T[0:1, :]


def to_column(row):
    return jnp.broadcast_to(row, (128, 128)).T[:, 0:1]


def kernel(
    q_in, k_in, v_in, cf_ref, att,
    qb, qp, kb, vb, cfb, cf_in, bias, held, held_max, op, op_in, st, st_in, ob,
    asend, arecv, alocal, gs, gr, hs, hr, os_, or_, rs, rr, rl,
):
    c, z, yh, xh, xl, co = (lax.axis_index(a) for a in AXES)
    g = yh * 2 + xh
    half = z // 4
    head = z * 4 + g

    def dev(c=c, z=z, g=g, xl=xl, co=co):
        return (c, z, g // 2, lax.rem(g, 2), xl, co)

    def gx(d):
        return ((yh + d // 2) % 2) * 2 + (xh + d % 2) % 2

    def zx(d):
        return lax.rem(z + d, 8)

    before = lax.rem(c + 3, 4)
    after = lax.rem(c + 1, 4)
    twin = dev(co=1 - co)
    across = dev(xl=1 - xl)

    far = sorted(
        ((d, e) for d in range(8) for e in range(4) if (d, e) != (0, 0)),
        key=lambda p: -(min(p[0], 8 - p[0]) + 4 * (p[1] // 2) + 2 * (p[1] % 2)),
    )
    barrier = pltpu.get_barrier_semaphore()
    partners = [dev(z=zx(d), g=gx(e)) for d, e in far]
    partners += [dev(c=before), dev(c=after), across, twin]
    for partner in partners:
        pl.semaphore_signal(barrier, inc=1, device_id=partner, device_id_type=MESH)
    for slot in range(4):
        vb[slot, :, :, :, :, HD:] = jnp.ones((2, 8, 4, 16, HD), jnp.bfloat16)
    cfb[...] = jnp.full((8, 128), cf_ref[0], jnp.float32)
    pl.semaphore_wait(barrier, len(partners))

    def remote(src, dst, send, recv, to):
        return pltpu.make_async_remote_copy(
            src_ref=src, dst_ref=dst, send_sem=send, recv_sem=recv, device_id=to, device_id_type=MESH
        )

    def lanes(start, size):
        return pl.ds(pl.multiple_of(start, 128), size)

    sent = []

    def exchange(n, rows, src, dst):
        for d, e in far:
            to_z, to_g = zx(d), gx(e)
            remote(
                src.at[rows, lanes((to_z * 4 + to_g) * HD, HD)], dst, asend.at[n], arecv.at[n], dev(z=to_z, g=to_g)
            ).start()
        pltpu.make_async_copy(src.at[rows, lanes(head * HD, HD)], dst, alocal.at[n]).start()

    def all_bytes(semaphore, rows=32):
        area = att.at[0:rows, pl.ds(0, len(far) * HD)]
        return pltpu.make_async_copy(area, area, semaphore)

    def arrived(n, rows=16):
        all_bytes(arecv.at[n], rows).wait()
        area = att.at[0:rows, pl.ds(0, HD)]
        pltpu.make_async_copy(area, area, alocal.at[n]).wait()

    def gather(n, part, buf):
        at = [buf.at[slot, part, :, :, :, cols] for slot in range(4)]
        to_twin = remote(at[0], at[1], gs.at[n, 0], gr.at[n, 0], twin)
        to_across = remote(at[0], at[2], gs.at[n, 1], gr.at[n, 1], across)
        relay = remote(at[2], at[3], gs.at[n, 2], gr.at[n, 2], twin)
        to_across.start()
        to_twin.start()
        sent.extend((to_twin, to_across, relay))
        return to_twin, to_across, relay

    cols = pl.ds(0, HD)
    for slot in range(4):
        vb[slot, :, :, :, :, HD:] = jnp.ones((2, 8, 4, 16, HD), jnp.bfloat16)
    @pl.when(c == 0)
    def _():
        op_in[...] = jnp.zeros_like(op_in)
        st_in[:, 0:4, :] = jnp.full((2, 4, 128), NEG, jnp.float32)
        st_in[:, 4:8, :] = jnp.zeros((2, 4, 128), jnp.float32)

    exchange(0, pl.ds(0, 32), q_in, qb.at[z, g])
    for part in range(2):
        rows = pl.ds(part * 16, 16)
        exchange(1 + 2 * part, rows, k_in, kb.at[0, part, z, g])
        exchange(2 + 2 * part, rows, v_in, vb.at[0, part, z, g, :, cols])

    arrived(0, 32)
    q_hop = remote(qb, qp, hs.at[0], hr.at[0], dev(c=before))
    cf_hop = remote(cfb, cf_in, hs.at[1], hr.at[1], dev(c=before))

    @pl.when(c > 0)
    def _():
        cf_hop.start()
        q_hop.start()

    here_0, here_1, there_0, there_1 = (((s, p), (s + 1, p)) for s in (0, 2) for p in (0, 1))

    def attend(queries, groups, masked, state=None):
        largest, numer = state if state else (None, None)
        for slot, part in groups:
            keys = kb[slot, part].reshape(512, HD)
            values = vb[slot, part].reshape(512, 2 * HD)
            scores = lax.dot_general(queries, keys, NT, preferred_element_type=jnp.float32)
            if masked:
                scores = scores + bias[slot : slot + 1, part * 512 : part * 512 + 512]
            top = jnp.max(scores, axis=1, keepdims=True)
            updated = top if largest is None else jnp.maximum(largest, top)
            weights = jnp.exp2((scores - updated) * LOG2).astype(jnp.bfloat16)
            more = jnp.dot(weights, values, preferred_element_type=jnp.float32)
            numer = more if largest is None else numer * jnp.exp2((largest - updated) * LOG2) + more
            largest = updated
        return largest, numer

    def hold(n, result):
        held_max[n] = jnp.broadcast_to(result[0], (512, 128))
        held[n] = result[1]

    def holding(n):
        return held_max[n][:, 0:1], held[n]

    def queries_of(buf, i):
        return buf[pl.ds(((half + 1 - i) % 2) * 4, 4)].reshape(512, HD)

    def past_more(groups):
        @pl.when(c < 3)
        def _():
            for i in range(2):
                hold(i, attend(queries_of(qp, i), groups, True, holding(i)))

    def returns(i):
        rows4 = pl.ds(((half + 1 - i) % 2) * 4, 4)
        return (
            remote(op.at[rows4], op_in.at[rows4], os_.at[i], or_.at[i], dev(c=after)),
            remote(st.at[i], st_in.at[i], os_.at[2 + i], or_.at[2 + i], dev(c=after)),
        )

    arrived(1)
    k0_twin, k0_across, k0_relay = gather(0, 0, kb)
    arrived(2)
    v0_twin, v0_across, v0_relay = gather(1, 0, vb)
    k0_across.wait_recv()
    k0_relay.start()
    k0_twin.wait_recv()
    v0_twin.wait_recv()
    hold(2, attend(queries_of(qb, 0), here_0, False))
    arrived(3)
    k1_twin, k1_across, k1_relay = gather(2, 1, kb)
    v0_across.wait_recv()
    v0_relay.start()

    @pl.when(c < 3)
    def _():
        q_hop.wait_recv()
        cf_hop.wait_recv()
        cache_from = cf_in[0:1, 0:1]
        for slot in range(4):
            chunk = lax.rem(xl + slot // 2, 2) * 2 + lax.rem(co + slot % 2, 2)
            row = lax.broadcasted_iota(jnp.int32, (1, 1024), 1)
            position = ((row % 512) // 16) * 128 + chunk * 32 + (row // 512) * 16 + row % 16
            bias[pl.ds(slot, 1), :] = jnp.where(position.astype(jnp.float32) >= cache_from, 0.0, NEG)
        for i in range(2):
            hold(i, attend(queries_of(qp, i), here_0, True))

    arrived(4)
    v1_twin, v1_across, v1_relay = gather(3, 1, vb)
    k0_relay.wait_recv()
    v0_relay.wait_recv()
    past_more(there_0)
    k1_across.wait_recv()
    k1_relay.start()
    k1_twin.wait_recv()
    v1_twin.wait_recv()
    past_more(here_1)
    v1_across.wait_recv()
    v1_relay.start()
    hold(3, attend(queries_of(qb, 1), here_0, False))
    k1_relay.wait_recv()
    v1_relay.wait_recv()

    @pl.when(c < 3)
    def _():
        for i in range(2):
            largest, numer = attend(queries_of(qp, i), there_1, True, holding(i))
            total = numer[:, HD : HD + 1]
            rows4 = pl.ds(((half + 1 - i) % 2) * 4, 4)
            op[rows4] = (numer[:, :HD] / total).astype(jnp.bfloat16).reshape(4, 4, 32, HD)
            for n in range(4):
                rows = slice(n * 128, n * 128 + 128)
                st[i, n : n + 1, :] = to_row(largest[rows])
                st[i, n + 4 : n + 5, :] = to_row(total[rows])
            for copy in returns(i):
                copy.start()

    for i in range(2):
        base = (half + 1 - i) % 2
        rows4 = pl.ds(base * 4, 4)
        largest, numer = attend(queries_of(qb, i), there_0 + here_1 + there_1, False, holding(2 + i))
        total = numer[:, HD : HD + 1]

        @pl.when(c > 0)
        def _():
            for copy in returns(i):
                copy.wait_recv()

        past = op_in[rows4].reshape(512, HD).astype(jnp.float32)
        past_largest = jnp.concatenate([to_column(st_in[i, n : n + 1, :]) for n in range(4)], 0)
        past_total = jnp.concatenate([to_column(st_in[i, n + 4 : n + 5, :]) for n in range(4)], 0)
        updated = jnp.maximum(largest, past_largest)
        mine = jnp.exp2((largest - updated) * LOG2)
        theirs = past_total * jnp.exp2((past_largest - updated) * LOG2)
        whole = (numer[:, :HD] * mine + past * theirs) / (total * mine + theirs)
        ob[rows4] = whole.astype(jnp.bfloat16).reshape(4, 4, 32, HD)
        for k in range(4):
            to_z = base * 4 + (z + k) % 4
            for e in (3, 2, 1, 0):
                to_g = gx(e)
                if i == 1 and k == 0 and e == 0:
                    continue
                remote(
                    ob.at[to_z, to_g], att.at[:, lanes(head * HD, HD)], rs.at[0], rr.at[0], dev(z=to_z, g=to_g)
                ).start()
    own = pltpu.make_async_copy(ob.at[z, g], att.at[:, lanes(head * HD, HD)], rl.at[0])
    own.start()
    own.wait()
    all_bytes(rr.at[0]).wait()
    all_bytes(rs.at[0]).wait()
    for n in range(5):
        all_bytes(asend.at[n], 16 if n else 32).wait()
    for copy in sent:
        copy.wait_send()

    @pl.when(c > 0)
    def _():
        q_hop.wait_send()
        cf_hop.wait_send()

    @pl.when(c < 3)
    def _():
        for i in range(2):
            for copy in returns(i):
                copy.wait_send()


def body(query_rows, key_rows, value_rows, cache_from, time_index, gate_table):
    bf16, f32, dma = jnp.bfloat16, jnp.float32, pltpu.SemaphoreType.DMA
    vmem = pl.BlockSpec(memory_space=pltpu.VMEM)
    hbm = pl.BlockSpec(memory_space=pltpu.HBM)
    attended = pl.pallas_call(
        kernel,
        out_shape=jax.ShapeDtypeStruct((32, HEADS * HD), bf16),
        in_specs=[hbm, hbm, hbm, pl.BlockSpec(memory_space=pltpu.SMEM)],
        out_specs=vmem,
        scratch_shapes=[
            *[pltpu.VMEM((8, 4, 32, HD), bf16)] * 2,
            pltpu.VMEM((4, 2, 8, 4, 16, HD), bf16),
            pltpu.VMEM((4, 2, 8, 4, 16, 2 * HD), bf16),
            *[pltpu.VMEM((8, 128), f32)] * 2,
            pltpu.VMEM((8, 1024), f32),
            pltpu.VMEM((4, 512, 2 * HD), f32),
            pltpu.VMEM((4, 512, 128), f32),
            *[pltpu.VMEM((8, 4, 32, HD), bf16)] * 2,
            *[pltpu.VMEM((2, 8, 128), f32)] * 2,
            pltpu.VMEM((8, 4, 32, HD), bf16),
            *[dma((5,))] * 3,
            *[dma((4, 3))] * 2,
            *[dma((2,))] * 2,
            *[dma((4,))] * 2,
            *[dma((1,))] * 3,
        ],
        compiler_params=pltpu.CompilerParams(
            collective_id=1, has_side_effects=True, vmem_limit_bytes=56_160_000
        ),
    )(query_rows[0], key_rows[0], value_rows[0], cache_from)
    gate_row = lax.dynamic_slice_in_dim(gate_table, time_index[0], 1, 0)
    return (attended.astype(jnp.float32) * gate_row).astype(jnp.bfloat16)[None]


def solution(mesh):
    finer = Mesh(mesh.devices.reshape(4, 8, 2, 2, 2, 2), AXES)
    rows = P("stretch", SEQ, None)
    return jax.shard_map(
        body,
        mesh=finer,
        in_specs=(rows, rows, rows, P("stretch"), P("stretch"), P()),
        out_specs=rows,
        check_vma=False,
    )
```

```python
import functools
import math

import jax
import jax.numpy as jnp
from jax import lax
from jax.experimental import pallas as pl
from jax.experimental.pallas import tpu as pltpu
from jax.sharding import Mesh
from jax.sharding import PartitionSpec as P

HEADS = 32
HD = 128
AXES = ("stretch", "z", "yh", "xh", "xl", "co")
SEQ = AXES[1:]
MESH = pl.DeviceIdType.MESH
NEG = -1e30
LOG2 = HD**-0.5 * math.log2(math.e)
NT = (((1,), (1,)), ((), ()))


def to_row(column):
    return jnp.broadcast_to(column, (128, 128)).T[0:1, :]


def to_column(row):
    return jnp.broadcast_to(row, (128, 128)).T[:, 0:1]


def kernel(
    q_in, k_in, v_in, cf_ref, att,
    qb, qp, kb, vb, cfb, cf_in, bias, held, held_max, op, op_in, st, st_in, ob,
    asend, arecv, alocal, gs, gr, hs, hr, os_, or_, rs, rr, rl,
):
    c, z, yh, xh, xl, co = (lax.axis_index(a) for a in AXES)
    g = yh * 2 + xh
    half = z // 4
    head = z * 4 + g

    def dev(c=c, z=z, g=g, xl=xl, co=co):
        return (c, z, g // 2, lax.rem(g, 2), xl, co)

    def gx(d):
        return ((yh + d // 2) % 2) * 2 + (xh + d % 2) % 2

    def zx(d):
        return lax.rem(z + d, 8)

    before = lax.rem(c + 3, 4)
    after = lax.rem(c + 1, 4)
    twin = dev(co=1 - co)
    across = dev(xl=1 - xl)

    far = sorted(
        ((d, e) for d in range(8) for e in range(4) if (d, e) != (0, 0)),
        key=lambda p: -(min(p[0], 8 - p[0]) + 4 * (p[1] // 2) + 2 * (p[1] % 2)),
    )
    barrier = pltpu.get_barrier_semaphore()
    partners = [dev(z=zx(d), g=gx(e)) for d, e in far]
    partners += [dev(c=before), dev(c=after), across, twin]
    for partner in partners:
        pl.semaphore_signal(barrier, inc=1, device_id=partner, device_id_type=MESH)
    for slot in range(4):
        vb[slot, :, :, :, :, HD:] = jnp.ones((2, 8, 4, 16, HD), jnp.bfloat16)
    cfb[...] = jnp.full((8, 128), cf_ref[0], jnp.float32)
    pl.semaphore_wait(barrier, len(partners))

    def remote(src, dst, send, recv, to):
        return pltpu.make_async_remote_copy(
            src_ref=src, dst_ref=dst, send_sem=send, recv_sem=recv, device_id=to, device_id_type=MESH
        )

    def lanes(start, size):
        return pl.ds(pl.multiple_of(start, 128), size)

    sent = []

    def exchange(n, rows, src, dst):
        for d, e in far:
            to_z, to_g = zx(d), gx(e)
            remote(
                src.at[rows, lanes((to_z * 4 + to_g) * HD, HD)], dst, asend.at[n], arecv.at[n], dev(z=to_z, g=to_g)
            ).start()
        pltpu.make_async_copy(src.at[rows, lanes(head * HD, HD)], dst, alocal.at[n]).start()

    def all_bytes(semaphore, rows=32):
        area = att.at[0:rows, pl.ds(0, len(far) * HD)]
        return pltpu.make_async_copy(area, area, semaphore)

    def arrived(n, rows=16):
        all_bytes(arecv.at[n], rows).wait()
        area = att.at[0:rows, pl.ds(0, HD)]
        pltpu.make_async_copy(area, area, alocal.at[n]).wait()

    def gather(n, part, buf):
        at = [buf.at[slot, part, :, :, :, cols] for slot in range(4)]
        to_twin = remote(at[0], at[1], gs.at[n, 0], gr.at[n, 0], twin)
        to_across = remote(at[0], at[2], gs.at[n, 1], gr.at[n, 1], across)
        relay = remote(at[2], at[3], gs.at[n, 2], gr.at[n, 2], twin)
        to_across.start()
        to_twin.start()
        sent.extend((to_twin, to_across, relay))
        return to_twin, to_across, relay

    cols = pl.ds(0, HD)
    for slot in range(4):
        vb[slot, :, :, :, :, HD:] = jnp.ones((2, 8, 4, 16, HD), jnp.bfloat16)
    @pl.when(c == 0)
    def _():
        op_in[...] = jnp.zeros_like(op_in)
        st_in[:, 0:4, :] = jnp.full((2, 4, 128), NEG, jnp.float32)
        st_in[:, 4:8, :] = jnp.zeros((2, 4, 128), jnp.float32)

    exchange(0, pl.ds(0, 32), q_in, qb.at[z, g])
    for part in range(2):
        rows = pl.ds(part * 16, 16)
        exchange(1 + 2 * part, rows, k_in, kb.at[0, part, z, g])
        exchange(2 + 2 * part, rows, v_in, vb.at[0, part, z, g, :, cols])

    arrived(0, 32)
    q_hop = remote(qb, qp, hs.at[0], hr.at[0], dev(c=before))
    cf_hop = remote(cfb, cf_in, hs.at[1], hr.at[1], dev(c=before))

    @pl.when(c > 0)
    def _():
        cf_hop.start()
        q_hop.start()

    here_0, here_1, there_0, there_1 = (((s, p), (s + 1, p)) for s in (0, 2) for p in (0, 1))

    def attend(queries, groups, masked, state=None):
        largest, numer = state if state else (None, None)
        for slot, part in groups:
            keys = kb[slot, part].reshape(512, HD)
            values = vb[slot, part].reshape(512, 2 * HD)
            scores = lax.dot_general(queries, keys, NT, preferred_element_type=jnp.float32)
            if masked:
                scores = scores + bias[slot : slot + 1, part * 512 : part * 512 + 512]
            top = jnp.max(scores, axis=1, keepdims=True)
            updated = top if largest is None else jnp.maximum(largest, top)
            weights = jnp.exp2((scores - updated) * LOG2).astype(jnp.bfloat16)
            more = jnp.dot(weights, values, preferred_element_type=jnp.float32)
            numer = more if largest is None else numer * jnp.exp2((largest - updated) * LOG2) + more
            largest = updated
        return largest, numer

    def hold(n, result):
        held_max[n] = jnp.broadcast_to(result[0], (512, 128))
        held[n] = result[1]

    def holding(n):
        return held_max[n][:, 0:1], held[n]

    def queries_of(buf, i):
        return buf[pl.ds(((half + 1 - i) % 2) * 4, 4)].reshape(512, HD)

    def past_more(groups):
        @pl.when(c < 3)
        def _():
            for i in range(2):
                hold(i, attend(queries_of(qp, i), groups, True, holding(i)))

    def returns(i):
        rows4 = pl.ds(((half + 1 - i) % 2) * 4, 4)
        return (
            remote(op.at[rows4], op_in.at[rows4], os_.at[i], or_.at[i], dev(c=after)),
            remote(st.at[i], st_in.at[i], os_.at[2 + i], or_.at[2 + i], dev(c=after)),
        )

    arrived(1)
    k0_twin, k0_across, k0_relay = gather(0, 0, kb)
    arrived(2)
    v0_twin, v0_across, v0_relay = gather(1, 0, vb)
    k0_across.wait_recv()
    k0_relay.start()
    k0_twin.wait_recv()
    v0_twin.wait_recv()
    hold(2, attend(queries_of(qb, 0), here_0, False))
    arrived(3)
    k1_twin, k1_across, k1_relay = gather(2, 1, kb)
    v0_across.wait_recv()
    v0_relay.start()

    @pl.when(c < 3)
    def _():
        q_hop.wait_recv()
        cf_hop.wait_recv()
        cache_from = cf_in[0:1, 0:1]
        for slot in range(4):
            chunk = lax.rem(xl + slot // 2, 2) * 2 + lax.rem(co + slot % 2, 2)
            row = lax.broadcasted_iota(jnp.int32, (1, 1024), 1)
            position = ((row % 512) // 16) * 128 + chunk * 32 + (row // 512) * 16 + row % 16
            bias[pl.ds(slot, 1), :] = jnp.where(position.astype(jnp.float32) >= cache_from, 0.0, NEG)
        for i in range(2):
            hold(i, attend(queries_of(qp, i), here_0, True))

    arrived(4)
    v1_twin, v1_across, v1_relay = gather(3, 1, vb)
    k0_relay.wait_recv()
    v0_relay.wait_recv()
    past_more(there_0)
    k1_across.wait_recv()
    k1_relay.start()
    k1_twin.wait_recv()
    v1_twin.wait_recv()
    past_more(here_1)
    v1_across.wait_recv()
    v1_relay.start()
    hold(3, attend(queries_of(qb, 1), here_0, False))
    k1_relay.wait_recv()
    v1_relay.wait_recv()

    @pl.when(c < 3)
    def _():
        for i in range(2):
            largest, numer = attend(queries_of(qp, i), there_1, True, holding(i))
            total = numer[:, HD : HD + 1]
            rows4 = pl.ds(((half + 1 - i) % 2) * 4, 4)
            op[rows4] = (numer[:, :HD] / total).astype(jnp.bfloat16).reshape(4, 4, 32, HD)
            for n in range(4):
                rows = slice(n * 128, n * 128 + 128)
                st[i, n : n + 1, :] = to_row(largest[rows])
                st[i, n + 4 : n + 5, :] = to_row(total[rows])
            for copy in returns(i):
                copy.start()

    for i in range(2):
        base = (half + 1 - i) % 2
        rows4 = pl.ds(base * 4, 4)
        largest, numer = attend(queries_of(qb, i), there_0 + here_1 + there_1, False, holding(2 + i))
        total = numer[:, HD : HD + 1]

        @pl.when(c > 0)
        def _():
            for copy in returns(i):
                copy.wait_recv()

        past = op_in[rows4].reshape(512, HD).astype(jnp.float32)
        past_largest = jnp.concatenate([to_column(st_in[i, n : n + 1, :]) for n in range(4)], 0)
        past_total = jnp.concatenate([to_column(st_in[i, n + 4 : n + 5, :]) for n in range(4)], 0)
        updated = jnp.maximum(largest, past_largest)
        mine = jnp.exp2((largest - updated) * LOG2)
        theirs = past_total * jnp.exp2((past_largest - updated) * LOG2)
        whole = (numer[:, :HD] * mine + past * theirs) / (total * mine + theirs)
        ob[rows4] = whole.astype(jnp.bfloat16).reshape(4, 4, 32, HD)
        for e in (3, 2, 1, 0):
            for k in (2, 1, 3, 0):
                to_z, to_g = base * 4 + (z + k) % 4, gx(e)
                if i == 1 and k == 0 and e == 0:
                    continue
                remote(
                    ob.at[to_z, to_g], att.at[:, lanes(head * HD, HD)], rs.at[0], rr.at[0], dev(z=to_z, g=to_g)
                ).start()
    own = pltpu.make_async_copy(ob.at[z, g], att.at[:, lanes(head * HD, HD)], rl.at[0])
    own.start()
    own.wait()
    all_bytes(rr.at[0]).wait()
    all_bytes(rs.at[0]).wait()
    for n in range(5):
        all_bytes(asend.at[n], 16 if n else 32).wait()
    for copy in sent:
        copy.wait_send()

    @pl.when(c > 0)
    def _():
        q_hop.wait_send()
        cf_hop.wait_send()

    @pl.when(c < 3)
    def _():
        for i in range(2):
            for copy in returns(i):
                copy.wait_send()


def body(query_rows, key_rows, value_rows, cache_from, time_index, gate_table):
    bf16, f32, dma = jnp.bfloat16, jnp.float32, pltpu.SemaphoreType.DMA
    vmem = pl.BlockSpec(memory_space=pltpu.VMEM)
    hbm = pl.BlockSpec(memory_space=pltpu.HBM)
    attended = pl.pallas_call(
        kernel,
        out_shape=jax.ShapeDtypeStruct((32, HEADS * HD), bf16),
        in_specs=[hbm, hbm, hbm, pl.BlockSpec(memory_space=pltpu.SMEM)],
        out_specs=vmem,
        scratch_shapes=[
            *[pltpu.VMEM((8, 4, 32, HD), bf16)] * 2,
            pltpu.VMEM((4, 2, 8, 4, 16, HD), bf16),
            pltpu.VMEM((4, 2, 8, 4, 16, 2 * HD), bf16),
            *[pltpu.VMEM((8, 128), f32)] * 2,
            pltpu.VMEM((8, 1024), f32),
            pltpu.VMEM((4, 512, 2 * HD), f32),
            pltpu.VMEM((4, 512, 128), f32),
            *[pltpu.VMEM((8, 4, 32, HD), bf16)] * 2,
            *[pltpu.VMEM((2, 8, 128), f32)] * 2,
            pltpu.VMEM((8, 4, 32, HD), bf16),
            *[dma((5,))] * 3,
            *[dma((4, 3))] * 2,
            *[dma((2,))] * 2,
            *[dma((4,))] * 2,
            *[dma((1,))] * 3,
        ],
        compiler_params=pltpu.CompilerParams(
            collective_id=1, has_side_effects=True, vmem_limit_bytes=56_160_000
        ),
    )(query_rows[0], key_rows[0], value_rows[0], cache_from)
    gate_row = lax.dynamic_slice_in_dim(gate_table, time_index[0], 1, 0)
    return (attended.astype(jnp.float32) * gate_row).astype(jnp.bfloat16)[None]


def solution(mesh):
    finer = Mesh(mesh.devices.reshape(4, 8, 2, 2, 2, 2), AXES)
    rows = P("stretch", SEQ, None)
    return jax.shard_map(
        body,
        mesh=finer,
        in_specs=(rows, rows, rows, P("stretch"), P("stretch"), P()),
        out_specs=rows,
        check_vma=False,
    )
```
